256 devices in a mesh: clus: 4 (over z_lo, core), sub: 64 (over x, z_hi, y).
Axes of the slice: x: 4, y: 4, z: 8 (z_hi: 4, z_lo: 2; z = z_hi * 2 + z_lo), core: 2. Of those that a mesh axis runs over, the one named last changes fastest.
Arguments:
- load: float32 [4, 64, 6, 256, 128], P('clus', 'sub'), may hold values from -30 to 30
- dual_op: float32 [4, 64, 1536, 1536], P('clus', 'sub'), may hold values from -6 to 17, as said below
- modes: float32 [4, 64, 32, 1536], P('clus', 'sub'), may hold values from -1 to 1
- face_map: int32 [4, 64, 3, 256], P('clus', 'sub'), may hold values from 0 to 255, each once within a row
- cluster: int32 [4, 64], P('clus', 'sub'), may hold values from 0 to 1, as said below
Outputs:
- multipliers: float32 [4, 64, 6, 256, 128], P('clus', 'sub')
- residual: float32 [4, 64, 6, 256, 128], P('clus', 'sub')
The draws below stay inside these ranges and needn't reach their ends.
Inputs may be any that keep to these rules, and one draw needn't show every extreme that they name: `dual_op`: each subdomain's block is symmetric positive definite. `face_map`: each row of 256 entries names every row of the neighbour's face once. In every cluster group exactly half of the 64 subdomains belong to each of its two clusters.
All inputs are finite; a program needn't handle non-finite values.
Results may differ from the reference program's by a relative error of at most 0.00011.
Values sent between devices are 32-bit elements; how exact they have to be, the bound alone decides.
No kernel may reach another device: no remote copies, remote signals or barrier semaphores. Data moves between devices by JAX's collectives and lax.ppermute only.
A program may use at most 128 MiB of HBM per device.

```python
import math
import jax
import jax.numpy as jnp
from jax import lax

FACE = 256
MODES = 32
COLS = 128
ITERS = 3
ORDER = 1536
GROUPS = 4
SUBS = 64


def mode_table(key):
    folded = jax.random.fold_in(key, 71)
    entries = jax.random.normal(folded, (GROUPS, SUBS, MODES, ORDER), jnp.float32)
    return jnp.clip(entries / math.sqrt(ORDER), -0.99, 0.99)


def draw_modes(key, part):
    return mode_table(key)


def draw_load(key, part):
    table = mode_table(key)
    folded = jax.random.fold_in(key, 5)
    noise_key, weight_key = jax.random.split(folded)
    noise = jax.random.normal(noise_key, (GROUPS, SUBS, ORDER, COLS), jnp.float32)
    weights = jax.random.normal(weight_key, (GROUPS, MODES, COLS), jnp.float32) * math.sqrt(ORDER / MODES)
    rising = 1.0 + 2.0 * jnp.arange(SUBS, dtype=jnp.float32) / max(SUBS - 1, 1)
    coarse_part = jnp.einsum('gsmn,gmc->gsnc', table, weights)
    result = noise * rising[None, :, None, None] + coarse_part
    return jnp.clip(result, -30.0, 30.0).reshape(GROUPS, SUBS, 6, FACE, COLS)


def draw_dual_op(key, part):
    folded = jax.random.fold_in(key, 13)
    block_keys = jax.random.split(folded, GROUPS * SUBS)

    def one_block(block_key):
        entry_key, diag_key = jax.random.split(block_key)
        entries = jax.random.normal(entry_key, (ORDER, ORDER), jnp.float32)
        symmetric = (entries + entries.T) * (0.25 / math.sqrt(ORDER))
        diagonal = jnp.exp(jax.random.uniform(diag_key, (ORDER,), jnp.float32, math.log(0.9), math.log(1.8)))
        return jnp.clip(symmetric, -0.9, 0.9) + jnp.diag(diagonal)
    blocks = lax.map(one_block, block_keys).reshape(GROUPS, SUBS, ORDER, ORDER)
    position = (jnp.arange(GROUPS, dtype=jnp.float32)[:, None] * SUBS + jnp.arange(SUBS, dtype=jnp.float32)[None, :]) / max(GROUPS * SUBS - 1, 1)
    scaling = 1.0 + 2.0 * position
    return blocks * scaling[:, :, None, None]


def draw_cluster(key, part):
    group_keys = jax.random.split(jax.random.fold_in(key, 29), GROUPS)

    def one_group(group_key):
        return (jax.random.permutation(group_key, SUBS) < SUBS // 2).astype(jnp.int32)
    return jax.vmap(one_group)(group_keys)


def setup_inputs(seed: int = 0) -> dict:
    key_of = jax.random.split(jax.random.key(seed), 6)
    load = draw_load(jax.random.fold_in(key_of[5], 71), 0)
    dual_op = draw_dual_op(jax.random.fold_in(key_of[5], 71), 0)
    modes = draw_modes(jax.random.fold_in(key_of[5], 71), 0)
    face_map = jax.vmap(lambda own: jax.random.permutation(own, FACE))(jax.random.split(key_of[3], GROUPS * SUBS * 3)).reshape((GROUPS, SUBS, 3, FACE)).astype(jnp.int32)
    cluster = draw_cluster(jax.random.fold_in(key_of[5], 71), 0)
    return {"load": load, "dual_op": dual_op, "modes": modes, "face_map": face_map, "cluster": cluster}


damping_factor = 0.8
highest = lax.Precision.HIGHEST

def owner_mask(face_map):
    plus_owned = face_map % 2 == 0
    minus_owned = jnp.broadcast_to(jnp.arange(face_map.shape[3]) % 2 == 1, plus_owned.shape)
    stacked = jnp.stack([plus_owned, minus_owned], axis=3)
    shape = face_map.shape
    return stacked.reshape(shape[0], shape[1], 6, shape[3], 1).astype(jnp.float32)

def partner(values, face_map, inverse):
    sub_count = values.shape[1]
    result = []
    for direction, (axis_index, shift_by) in enumerate(((1, 1), (0, 1), (1, sub_count // 2))):
        plus_face = values[:, :, 2 * direction]
        minus_face = values[:, :, 2 * direction + 1]
        pairing = face_map[:, :, direction]
        inverse_rows = inverse[:, :, direction]
        from_plus = jnp.roll(minus_face, -shift_by, axis=axis_index)
        plus_side = jnp.take_along_axis(from_plus, pairing[..., None], axis=2)
        from_minus = jnp.roll(plus_face, shift_by, axis=axis_index)
        minus_index = jnp.roll(inverse_rows, shift_by, axis=axis_index)
        minus_side = jnp.take_along_axis(from_minus, minus_index[..., None], axis=2)
        result += [plus_side, minus_side]
    return jnp.stack(result, axis=2)

def solve_one(lower_part, column_block):
    return jax.scipy.linalg.cho_solve((lower_part, True), column_block)

def reference(load, dual_op, modes, face_map, cluster):
    group_count, sub_count, face_count, face_rows, columns = load.shape
    order_rows = face_count * face_rows
    inverse = jnp.argsort(face_map, axis=-1).astype(jnp.int32)
    owned = owner_mask(face_map)
    owned_rows = owned.reshape(group_count, sub_count, 1, order_rows)
    selector = jax.nn.one_hot(cluster, 2, dtype=jnp.float32)
    gram_terms = jnp.einsum('gsmn,gskn->gsmk', modes * owned_rows, modes, precision=highest)
    coarse = jnp.einsum('gsc,gsmk->gcmk', selector, gram_terms, precision=highest)
    factor = jnp.linalg.cholesky(coarse)
    residual = load * owned
    multipliers = jnp.zeros_like(load)
    for iteration in range(ITERS):
        flat_rows = residual.reshape(group_count, sub_count, order_rows, columns)
        projected = jnp.einsum('gsmn,gsnc->gsmc', modes, flat_rows, precision=highest)
        gathered = jnp.einsum('gsc,gsmk->gcmk', selector, projected, precision=highest)
        coefficients = jax.vmap(jax.vmap(solve_one))(factor, gathered)
        own_coeff = jnp.einsum('gsc,gcmk->gsmk', selector, coefficients, precision=highest)
        correction = jnp.einsum('gsmn,gsmc->gsnc', modes, own_coeff, precision=highest).reshape(load.shape)
        search = residual - owned * correction
        numerator = jnp.sum(residual * search, axis=(0, 1, 2, 3))
        local_copy = search - (1.0 - owned) * partner(search, face_map, inverse)
        applied = jnp.einsum('gsnk,gskc->gsnc', dual_op, local_copy.reshape(group_count, sub_count, order_rows, columns), precision=highest).reshape(load.shape)
        assembled = owned * (applied - partner(applied, face_map, inverse))
        denominator = jnp.sum(search * assembled, axis=(0, 1, 2, 3))
        step_size = damping_factor * numerator / denominator
        multipliers = multipliers + step_size * search
        residual = residual - step_size * assembled
    return (multipliers, residual)
```

```python
import jax
import jax.numpy as jnp
from jax import lax
from jax.experimental import pallas as pl
from jax.experimental.pallas import tpu as pltpu
from jax.sharding import PartitionSpec as P

FACE = 256
HALF = 128
COLS = 128
MODES = 32
ORDER = 1536
FACES = 6
VMEM_LIMIT = 16 << 20
PACK = HALF + MODES + 8

damping_factor = 0.8
f32 = jnp.float32
bf16 = jnp.bfloat16


def exact_dot(a, b, contract=((1,), (0,))):
    return lax.dot_general(
        a, b, (contract, ((), ())), precision=lax.Precision.HIGHEST, preferred_element_type=f32
    )


def fast_dot(a, b, contract=((1,), (0,))):
    return lax.dot_general(a, b, (contract, ((), ())), preferred_element_type=f32)


def split3(x):
    high = x.astype(bf16)
    rest = x - high.astype(f32)
    middle = rest.astype(bf16)
    low = (rest - middle.astype(f32)).astype(bf16)
    return high, middle, low


def reorder(onehot, x):
    high, middle, low = split3(x)
    return fast_dot(onehot, high) + fast_dot(onehot, middle) + fast_dot(onehot, low)


def rows_of(side):
    return pl.ds(pl.multiple_of(side * HALF, HALF), HALF)


def is_owned(shape, axis, side):
    return lax.broadcasted_iota(jnp.int32, shape, axis) // HALF == side


def split_kernel(operator, high, low):
    values = operator[...]
    rounded = values.astype(bf16)
    high[0] = rounded
    low[0] = (values - rounded.astype(f32)).astype(bf16)


def setup_kernel(load, modes, onehot, own, face_of, load_p, modes_p, pack0, pack1, pack2, pack3, pack45, payload, packs):
    def one(slot, carry):
        gram, projected = carry
        face = face_of[slot]
        side = lax.rem(face, 2)
        load_p[slot] = reorder(onehot[slot], load[face])
        parts = split3(modes[:, pl.ds(pl.multiple_of(face * FACE, FACE), FACE)])
        rows = sum(fast_dot(part, onehot[slot], ((1,), (1,))) for part in parts)
        modes_p[slot] = rows
        mine = jnp.where(jnp.full((MODES, HALF), side) == 0, rows[:, :HALF], rows[:, HALF:])
        values = load_p[slot, rows_of(side)]
        packs[slot, 0:HALF] = values
        packs[slot, HALF : HALF + MODES] = mine
        packs[slot, HALF + MODES : PACK] = own[...]
        return gram + exact_dot(mine, mine, ((1,), (1,))), projected + exact_dot(mine, values)

    gram, projected = lax.fori_loop(
        0, FACES, one, (jnp.zeros((MODES, MODES), f32), jnp.zeros((MODES, COLS), f32))
    )
    for slot, pack in enumerate((pack0, pack1, pack2, pack3, pack45.at[0], pack45.at[1])):
        pack[...] = packs[slot]
    own_row = own[0:1]
    payload[0:MODES] = jnp.where(own_row == 0.0, projected, 0.0)
    payload[MODES : 2 * MODES] = jnp.where(own_row == 1.0, projected, 0.0)
    lane = lax.broadcasted_iota(jnp.int32, (MODES, COLS), 1)
    row = lax.broadcasted_iota(jnp.int32, (MODES, COLS), 0)
    place = (lane == row + MODES * own_row.astype(jnp.int32)).astype(f32)
    payload[2 * MODES : 3 * MODES] = exact_dot(gram, place)


def solve_both(inverses, gathered, own_row, coeff, own_coeff):
    zero = jnp.zeros((MODES, COLS), f32)
    first = exact_dot(inverses, jnp.concatenate([zero, zero, gathered[0:MODES], zero], axis=0))
    second = exact_dot(inverses, jnp.concatenate([zero, zero, zero, gathered[MODES : 2 * MODES]], axis=0))
    coeff[0:MODES] = first
    coeff[MODES : 2 * MODES] = second
    own_coeff[...] = jnp.where(own_row == 0.0, first, second)


def invert_kernel(sum0, sum1, sum2, sum3, own, inverses, gathered, coeff, own_coeff):
    reduced = (sum0[...] + sum1[...]) + (sum2[...] + sum3[...])
    lane = lax.broadcasted_iota(jnp.int32, (MODES, COLS), 1)
    row = lax.broadcasted_iota(jnp.int32, (MODES, COLS), 0)
    work = reduced[2 * MODES : 3 * MODES]
    work = jnp.where(lane < 2 * MODES, work, (lane % MODES == row).astype(f32))
    second = (lane // MODES) % 2 == 1
    for step in range(MODES):
        column = jnp.where(
            second,
            jnp.broadcast_to(work[:, MODES + step : MODES + step + 1], (MODES, COLS)),
            jnp.broadcast_to(work[:, step : step + 1], (MODES, COLS)),
        )
        scaled = work[step : step + 1] / column[step : step + 1]
        work = jnp.where(row == step, scaled, work - column * scaled)
    inverses[...] = work
    gathered[...] = reduced[0 : 2 * MODES]
    solve_both(work, reduced[0 : 2 * MODES], own[0:1], coeff, own_coeff)


def combine_kernel(partial, got2, got3, across, own, payload):
    arrived = got2[...] + got3[...]
    own_row = own[0:1]
    for slot in range(2):
        rows = slice(slot * MODES, (slot + 1) * MODES)
        payload[rows] = partial[rows] + jnp.where(own_row == slot, arrived[0:MODES], 0.0)
    tail = slice(2 * MODES, 2 * MODES + 8)
    payload[tail] = (partial[tail] + across[...]) + arrived[MODES : MODES + 8]


def step_kernel(sum0, sum1, sum2, sum3, gathered, inverses, own, alpha, gathered_out, coeff, own_coeff):
    reduced = (sum0[...] + sum1[...]) + (sum2[...] + sum3[...])
    step_size = damping_factor * reduced[64:65] / reduced[65:66]
    alpha[...] = jnp.broadcast_to(step_size, (8, COLS))
    updated = gathered[0 : 2 * MODES] - step_size * reduced[0 : 2 * MODES]
    gathered_out[...] = updated
    solve_both(inverses[...], updated, own[0:1], coeff, own_coeff)


def search_and_apply(face_of, residual, basis, ids, coeff, coeff2, coeff3, onehot, back, high, low, search, rhs, stacked, product):
    own_row = ids[6:7]
    own = jnp.where(own_row == 0.0, coeff[0:MODES], coeff[MODES : 2 * MODES])
    for slot in range(FACES):
        stacked[slot, 0:MODES] = own
        if slot == 2:
            other = coeff2[...]
        elif slot == 3:
            other = coeff3[...]
        else:
            other = jnp.where(ids[slot : slot + 1] == 0.0, coeff[0:MODES], coeff[MODES : 2 * MODES])
        stacked[slot, MODES : 2 * MODES] = other

    def one(slot, numerator):
        face = face_of[slot]
        values = residual[slot]
        found = values - exact_dot(basis[slot], stacked[slot], ((0,), (0,)))
        search[slot] = found
        top = found.astype(bf16)
        rest = (found - top.astype(f32)).astype(bf16)
        local = fast_dot(back[slot], jnp.concatenate([top, rest], axis=1))
        rhs[pl.ds(pl.multiple_of(face * FACE, FACE), FACE)] = local.astype(bf16)
        owned = is_owned((FACE, COLS), 0, lax.rem(face, 2))
        return numerator + jnp.sum(jnp.where(owned, values * found, 0.0), axis=0, keepdims=True)

    numerator = lax.fori_loop(0, FACES, one, jnp.zeros((1, COLS), f32))

    def two(slot, denominator):
        face = face_of[slot]
        both = fast_dot(high[face], rhs[...]) + fast_dot(low[face], rhs[...])
        found = reorder(onehot[slot], both[:, 0:COLS] + both[:, COLS : 2 * COLS])
        product[slot] = found
        return denominator + jnp.sum(search[slot] * found, axis=0, keepdims=True)

    denominator = lax.fori_loop(0, FACES, two, jnp.zeros((1, COLS), f32))
    return jnp.concatenate([numerator, denominator, jnp.zeros((6, COLS), f32)], axis=0)


def share_out(basis, ids, product, scalars, stacked, applied, partial, to2, to3, scal):
    def one(slot, carry):
        stacked[slot] = exact_dot(basis[slot], product[slot])
        return carry

    lax.fori_loop(0, FACES, one, 0)
    for slot in range(FACES):
        applied[slot][...] = product[slot]
    own_share = stacked[0, 0:MODES]
    for slot in range(1, FACES):
        own_share += stacked[slot, 0:MODES]
    for cluster in range(2):
        term = jnp.where(ids[6:7] == cluster, own_share, 0.0)
        for slot in (0, 1, 4, 5):
            term += jnp.where(ids[slot : slot + 1] == cluster, stacked[slot, MODES : 2 * MODES], 0.0)
        partial[cluster * MODES : (cluster + 1) * MODES] = term
    partial[2 * MODES : 2 * MODES + 8] = scalars
    to2[0:MODES] = stacked[2, MODES : 2 * MODES]
    to2[MODES : MODES + 8] = scalars
    to3[0:MODES] = stacked[3, MODES : 2 * MODES]
    to3[MODES : MODES + 8] = scalars
    scal[...] = scalars


def first_kernel(
    face_of, load_p, modes_p, got0, got1, got2, got3, got45, own, coeff, coeff2, coeff3, onehot, back, high, low,
    residual, basis, ids, search, ap0, ap1, ap2, ap3, ap45, partial, to2, to3, scal, rhs, stacked, product,
):
    got = (got0, got1, got2, got3, got45.at[1], got45.at[0])
    ids[6:8] = own[0:2]
    for slot in range(FACES):
        side = lax.rem(face_of[slot], 2)
        residual[slot, rows_of(side)] = load_p[slot, rows_of(side)]
        residual[slot, rows_of(1 - side)] = -got[slot][0:HALF]
        owned = is_owned((MODES, FACE), 1, side)
        theirs = got[slot][HALF : HALF + MODES]
        basis[slot, 0:MODES] = jnp.where(owned, modes_p[slot], 0.0)
        basis[slot, MODES : 2 * MODES] = jnp.where(owned, 0.0, -jnp.concatenate([theirs, theirs], axis=1))
        ids[slot : slot + 1] = got[slot][HALF + MODES : HALF + MODES + 1]
    scalars = search_and_apply(
        face_of, residual, basis, ids, coeff, coeff2, coeff3, onehot, back, high, low, search, rhs, stacked, product
    )
    applied = (ap0, ap1, ap2, ap3, ap45.at[0], ap45.at[1])
    share_out(basis, ids, product, scalars, stacked, applied, partial, to2, to3, scal)


def update(residual_in, search_in, total_in, applied_in, got, alpha, residual, total):
    step_size = alpha[0:1]
    for slot in range(FACES):
        residual[slot] = residual_in[slot] - step_size * (applied_in[slot][...] - got[slot][...])
        moved = step_size * search_in[slot]
        total[slot] = moved if total_in is None else total_in[slot] + moved


def middle_kernel(
    face_of, residual_in, search_in, in0, in1, in2, in3, in45, got0, got1, got2, got3, got45, alpha,
    basis, ids, coeff, coeff2, coeff3, onehot, back, high, low,
    residual, total, search, ap0, ap1, ap2, ap3, ap45, partial, to2, to3, scal, rhs, stacked, product,
):
    got = (got0, got1, got2, got3, got45.at[1], got45.at[0])
    applied_in = (in0, in1, in2, in3, in45.at[0], in45.at[1])
    update(residual_in, search_in, None, applied_in, got, alpha, residual, total)
    scalars = search_and_apply(
        face_of, residual, basis, ids, coeff, coeff2, coeff3, onehot, back, high, low, search, rhs, stacked, product
    )
    applied = (ap0, ap1, ap2, ap3, ap45.at[0], ap45.at[1])
    share_out(basis, ids, product, scalars, stacked, applied, partial, to2, to3, scal)


def last_kernel(
    face_of, residual_in, search_in, total_in, in0, in1, in2, in3, in45, got0, got1, got2, got3, got45, alpha,
    basis, ids, coeff, coeff2, coeff3, onehot, back, high, low,
    residual, total, search, product, ap0, ap1, ap2, ap3, ap45, scal, rhs, stacked,
):
    got = (got0, got1, got2, got3, got45.at[1], got45.at[0])
    applied_in = (in0, in1, in2, in3, in45.at[0], in45.at[1])
    update(residual_in, search_in, total_in, applied_in, got, alpha, residual, total)
    scal[...] = search_and_apply(
        face_of, residual, basis, ids, coeff, coeff2, coeff3, onehot, back, high, low, search, rhs, stacked, product
    )
    for slot, sent in enumerate((ap0, ap1, ap2, ap3, ap45.at[0], ap45.at[1])):
        sent[...] = product[slot, rows_of(1 - lax.rem(face_of[slot], 2))]


def finish_kernel(
    face_of, residual_in, search_in, total_in, product, got0, got1, got2, got3, got45, sum0, sum1, sum2, sum3, back,
    total, residual, arrived,
):
    reduced = (sum0[...] + sum1[...]) + (sum2[...] + sum3[...])
    step_size = damping_factor * reduced[0:1] / reduced[1:2]
    for slot, values in enumerate((got0, got1, got2, got3, got45.at[1], got45.at[0])):
        arrived[slot] = jnp.concatenate([values[...], values[...]], axis=0)

    def one(slot, carry):
        face = face_of[slot]
        owned = is_owned((FACE, COLS), 0, lax.rem(face, 2))
        summed = total_in[slot] + step_size * search_in[slot]
        left = residual_in[slot] - step_size * (product[slot] - arrived[slot])
        total[face] = reorder(back[slot], jnp.where(owned, summed, 0.0))
        residual[face] = reorder(back[slot], jnp.where(owned, left, 0.0))
        return carry

    lax.fori_loop(0, FACES, one, 0)


in_vmem = pl.BlockSpec(memory_space=pltpu.VMEM)
in_smem = pl.BlockSpec(memory_space=pltpu.SMEM)


def call(kernel, args, outs, scratch=(), scalars=()):
    shapes = [out if isinstance(out, jax.ShapeDtypeStruct) else jax.ShapeDtypeStruct(out, f32) for out in outs]
    return pl.pallas_call(
        kernel,
        out_shape=shapes,
        in_specs=[in_smem if arg.dtype == jnp.int32 else in_vmem for arg in args],
        out_specs=[in_vmem for _ in shapes],
        scratch_shapes=list(scratch),
        compiler_params=pltpu.CompilerParams(vmem_limit_bytes=VMEM_LIMIT),
        name=kernel.__name__,
    )(*args)


def permuted(array, axis, target):
    return lax.ppermute(array, axis, [(i, target(i)) for i in range(lax.axis_size(axis))])


def flipped(array, axis, mask):
    return permuted(array, axis, lambda i: i ^ mask)


def terms_over_sub(array):
    count = lax.axis_size("sub")
    stride = 1
    while True:
        block = 4 * stride
        terms = [array] + [
            permuted(array, "sub", lambda i, turn=turn: i - i % block + (i % block + turn * stride) % block)
            for turn in (1, 2, 3)
        ]
        if block == count:
            return terms
        array = (terms[0] + terms[1]) + (terms[2] + terms[3])
        stride = block


def exchange(sent0, sent1, sent2, sent3, sent45):
    count = lax.axis_size("sub")
    return (
        flipped(sent0, "sub", 1),
        permuted(sent1, "sub", lambda i: (i + 2 * (i % 2) - 1) % count),
        flipped(sent2, "clus", 1),
        flipped(sent3, "clus", 3),
        flipped(sent45, "sub", count // 2),
    )


def per_device(load, dual_op, modes, face_map, cluster):
    pairing = face_map[0, 0]
    odd_sub = lax.axis_index("sub") % 2
    odd_clus = lax.axis_index("clus") % 2
    face_of = jnp.stack(
        [odd_sub, 1 - odd_sub, 2 + odd_clus, 3 - odd_clus, jnp.int32(4), jnp.int32(5)]
    ).astype(jnp.int32)
    own = jnp.broadcast_to(cluster.astype(f32), (8, COLS))
    position = jnp.arange(FACE)
    natural = jnp.where(position < HALF, 2 * position, 2 * position - FACE + 1)
    plus_rows = pairing[jnp.array([0, 0, 1, 1, 2, 2])]
    rows = jnp.where((face_of % 2 == 0)[:, None], plus_rows, position[None])
    onehot = (rows[:, None, :] == natural[None, :, None]).astype(bf16)
    back = (rows[:, :, None] == natural[None, None, :]).astype(bf16)

    split = jax.ShapeDtypeStruct((FACES, FACE, ORDER), bf16)
    wide, narrow = (FACES, FACE, COLS), (PACK, HALF)
    load_p, modes_p, *packs, payload = call(
        setup_kernel,
        (load[0, 0], modes[0, 0], onehot, own, face_of),
        [wide, (FACES, MODES, FACE), narrow, narrow, narrow, narrow, (2, *narrow), (3 * MODES, COLS)],
        [pltpu.VMEM((FACES, *narrow), f32)],
    )
    high, low = pl.pallas_call(
        split_kernel,
        out_shape=[split, split],
        grid=(FACES,),
        in_specs=[pl.BlockSpec((FACE, ORDER), lambda i: (i, 0))],
        out_specs=[pl.BlockSpec((1, FACE, ORDER), lambda i: (i, 0, 0))] * 2,
        compiler_params=pltpu.CompilerParams(vmem_limit_bytes=VMEM_LIMIT),
        name="split_kernel",
    )(dual_op[0, 0])
    got = exchange(*packs)
    coeff_shape, one = (2 * MODES, COLS), (MODES, COLS)
    inverses, gathered, coeff, own_coeff = call(
        invert_kernel, (*terms_over_sub(payload), own), [one, coeff_shape, coeff_shape, one]
    )
    coeff2, coeff3 = flipped(own_coeff, "clus", 1), flipped(own_coeff, "clus", 3)

    face = (FACE, COLS)
    faces = [face, face, face, face, (2, *face)]
    sums = [(2 * MODES + 8, COLS), (MODES + 8, COLS), (MODES + 8, COLS), (8, COLS)]
    scratch = [
        pltpu.VMEM((ORDER, 2 * COLS), bf16),
        pltpu.VMEM((FACES, 2 * MODES, COLS), f32),
        pltpu.VMEM(wide, f32),
    ]
    residual, basis, ids, search, *rest = call(
        first_kernel,
        (face_of, load_p, modes_p, *got, own, coeff, coeff2, coeff3, onehot, back, high, low),
        [wide, (FACES, 2 * MODES, FACE), (8, COLS), wide, *faces, *sums],
        scratch,
    )
    total = None
    for iteration in (1, 2):
        applied, (partial, to2, to3, scal) = rest[:5], rest[5:]
        got2, got3, across = flipped(to2, "clus", 1), flipped(to3, "clus", 3), flipped(scal, "clus", 2)
        got = exchange(*applied)
        (payload,) = call(combine_kernel, (partial, got2, got3, across, own), [sums[0]])
        alpha, gathered, coeff, own_coeff = call(
            step_kernel,
            (*terms_over_sub(payload), gathered, inverses, own),
            [(8, COLS), coeff_shape, coeff_shape, one],
        )
        coeff2, coeff3 = flipped(own_coeff, "clus", 1), flipped(own_coeff, "clus", 3)
        common = (*applied, *got, alpha, basis, ids, coeff, coeff2, coeff3, onehot, back, high, low)
        if iteration == 1:
            residual, total, search, *rest = call(
                middle_kernel, (face_of, residual, search, *common), [wide, wide, wide, *faces, *sums], scratch
            )
        else:
            half = (HALF, COLS)
            residual, total, search, product, *rest = call(
                last_kernel,
                (face_of, residual, search, total, *common),
                [wide, wide, wide, wide, half, half, half, half, (2, *half), (8, COLS)],
                scratch[:2],
            )
    got = exchange(*rest[:5])
    scal = rest[5]
    scal = scal + flipped(scal, "clus", 1)
    scal = scal + flipped(scal, "clus", 2)
    total, residual = call(
        finish_kernel,
        (face_of, residual, search, total, product, *got, *terms_over_sub(scal), back),
        [wide, wide],
        [pltpu.VMEM(wide, f32)],
    )
    return (total[None, None], residual[None, None])


def solution(mesh):
    placed = (
        P("clus", "sub", None, None, None),
        P("clus", "sub", None, None),
        P("clus", "sub", None, None),
        P("clus", "sub", None, None),
        P("clus", "sub"),
    )
    return jax.shard_map(
        per_device,
        mesh=mesh,
        in_specs=placed,
        out_specs=(P("clus", "sub", None, None, None), P("clus", "sub", None, None, None)),
        check_vma=False,
    )
```

```python
import jax
import jax.numpy as jnp
from jax import lax
from jax.experimental import pallas as pl
from jax.experimental.pallas import tpu as pltpu
from jax.sharding import PartitionSpec as P

FACE = 256
HALF = 128
COLS = 128
MODES = 32
ORDER = 1536
FACES = 6
VMEM_LIMIT = 16 << 20
CHUNK = 768
PACK = HALF + MODES + 8

damping_factor = 0.8
f32 = jnp.float32
bf16 = jnp.bfloat16


def exact_dot(a, b, contract=((1,), (0,))):
    return lax.dot_general(
        a, b, (contract, ((), ())), precision=lax.Precision.HIGHEST, preferred_element_type=f32
    )


def fast_dot(a, b, contract=((1,), (0,))):
    return lax.dot_general(a, b, (contract, ((), ())), preferred_element_type=f32)


def split3(x):
    high = x.astype(bf16)
    rest = x - high.astype(f32)
    middle = rest.astype(bf16)
    low = (rest - middle.astype(f32)).astype(bf16)
    return high, middle, low


def reorder(onehot, x):
    high, middle, low = split3(x)
    return fast_dot(onehot, high) + fast_dot(onehot, middle) + fast_dot(onehot, low)


def rows_of(side):
    return pl.ds(pl.multiple_of(side * HALF, HALF), HALF)


def is_owned(shape, axis, side):
    return lax.broadcasted_iota(jnp.int32, shape, axis) // HALF == side


def faces_of_slots():
    odd_sub = lax.rem(lax.axis_index("sub"), 2)
    odd_clus = lax.rem(lax.axis_index("clus"), 2)
    return [odd_sub, 1 - odd_sub, 2 + odd_clus, 3 - odd_clus, 4, 5]


def split_kernel(operator, high, low):
    values = operator[...]
    rounded = values.astype(bf16)
    high[...] = rounded
    low[...] = (values - rounded.astype(f32)).astype(bf16)


def setup_kernel(
    cluster, load, modes, pairing, onehot, own, load_p, modes_p, pack0, pack1, pack2, pack3, pack45, payload, packs
):
    face_of = faces_of_slots()
    own[...] = jnp.full((8, COLS), cluster[0, 0]).astype(f32)
    row = lax.broadcasted_iota(jnp.int32, (FACE, FACE), 0)
    lane = lax.broadcasted_iota(jnp.int32, (FACE, FACE), 1)
    natural = jnp.where(row < HALF, 2 * row, 2 * row - FACE + 1)

    def one(slot, carry):
        gram, projected = carry
        face = face_of[slot]
        side = lax.rem(face, 2)
        plus = jnp.broadcast_to(pairing[slot // 2 : slot // 2 + 1], (FACE, FACE))
        target = jnp.where(jnp.full((FACE, FACE), side) == 0, plus, lane)
        onehot[slot] = (target == natural).astype(bf16)
        load_p[slot] = reorder(onehot[slot], load[face])
        parts = split3(modes[:, pl.ds(pl.multiple_of(face * FACE, FACE), FACE)])
        rows = sum(fast_dot(part, onehot[slot], ((1,), (1,))) for part in parts)
        modes_p[slot] = rows
        mine = jnp.where(jnp.full((MODES, HALF), side) == 0, rows[:, :HALF], rows[:, HALF:])
        values = load_p[slot, rows_of(side)]
        packs[slot, 0:HALF] = values
        packs[slot, HALF : HALF + MODES] = mine
        packs[slot, HALF + MODES : PACK] = own[...]
        return gram + exact_dot(mine, mine, ((1,), (1,))), projected + exact_dot(mine, values)

    gram, projected = jnp.zeros((MODES, MODES), f32), jnp.zeros((MODES, COLS), f32)
    for slot in range(FACES):
        gram, projected = one(slot, (gram, projected))
    for slot, pack in enumerate((pack0, pack1, pack2, pack3, pack45.at[0], pack45.at[1])):
        pack[...] = packs[slot]
    own_row = own[0:1]
    payload[0:MODES] = jnp.where(own_row == 0.0, projected, 0.0)
    payload[MODES : 2 * MODES] = jnp.where(own_row == 1.0, projected, 0.0)
    lane = lax.broadcasted_iota(jnp.int32, (MODES, COLS), 1)
    row = lax.broadcasted_iota(jnp.int32, (MODES, COLS), 0)
    place = (lane == row + MODES * own_row.astype(jnp.int32)).astype(f32)
    payload[2 * MODES : 3 * MODES] = exact_dot(gram, place)


def solve_both(inverses, gathered, own_row, coeff, own_coeff):
    zero = jnp.zeros((MODES, COLS), f32)
    first = exact_dot(inverses, jnp.concatenate([zero, zero, gathered[0:MODES], zero], axis=0))
    second = exact_dot(inverses, jnp.concatenate([zero, zero, zero, gathered[MODES : 2 * MODES]], axis=0))
    coeff[0:MODES] = first
    coeff[MODES : 2 * MODES] = second
    own_coeff[...] = jnp.where(own_row == 0.0, first, second)


def invert_kernel(sum0, sum1, sum2, sum3, own, inverses, gathered, coeff, own_coeff):
    reduced = (sum0[...] + sum1[...]) + (sum2[...] + sum3[...])
    lane = lax.broadcasted_iota(jnp.int32, (MODES, COLS), 1)
    row = lax.broadcasted_iota(jnp.int32, (MODES, COLS), 0)
    work = reduced[2 * MODES : 3 * MODES]
    work = jnp.where(lane < 2 * MODES, work, (lane % MODES == row).astype(f32))
    second = (lane // MODES) % 2 == 1
    for step in range(MODES):
        column = jnp.where(
            second,
            jnp.broadcast_to(work[:, MODES + step : MODES + step + 1], (MODES, COLS)),
            jnp.broadcast_to(work[:, step : step + 1], (MODES, COLS)),
        )
        scaled = work[step : step + 1] / column[step : step + 1]
        work = jnp.where(row == step, scaled, work - column * scaled)
    inverses[...] = work
    gathered[...] = reduced[0 : 2 * MODES]
    solve_both(work, reduced[0 : 2 * MODES], own[0:1], coeff, own_coeff)


def combine_kernel(partial, got2, got3, across, own, payload):
    arrived = got2[...] + got3[...]
    own_row = own[0:1]
    for slot in range(2):
        rows = slice(slot * MODES, (slot + 1) * MODES)
        payload[rows] = partial[rows] + jnp.where(own_row == slot, arrived[0:MODES], 0.0)
    tail = slice(2 * MODES, 2 * MODES + 8)
    payload[tail] = (partial[tail] + across[...]) + arrived[MODES : MODES + 8]


def step_kernel(sum0, sum1, sum2, sum3, gathered, inverses, own, alpha, gathered_out, coeff, own_coeff):
    reduced = (sum0[...] + sum1[...]) + (sum2[...] + sum3[...])
    step_size = damping_factor * reduced[64:65] / reduced[65:66]
    alpha[...] = jnp.broadcast_to(step_size, (8, COLS))
    updated = gathered[0 : 2 * MODES] - step_size * reduced[0 : 2 * MODES]
    gathered_out[...] = updated
    solve_both(inverses[...], updated, own[0:1], coeff, own_coeff)


def halves(x):
    top = x.astype(bf16)
    return top, (x - top.astype(f32)).astype(bf16)


def search_and_apply(
    residual, lift, fold, ids, coeff, coeff2, coeff3, onehot, back, high, low, search, rhs, local_product, shares, product
):
    face_of = faces_of_slots()
    own_row = ids[6:7]
    own = jnp.where(own_row == 0.0, coeff[0:MODES], coeff[MODES : 2 * MODES])
    numerator = jnp.zeros((1, COLS), f32)
    for slot in range(FACES):
        if slot == 2:
            other = coeff2[...]
        elif slot == 3:
            other = coeff3[...]
        else:
            other = jnp.where(ids[slot : slot + 1] == 0.0, coeff[0:MODES], coeff[MODES : 2 * MODES])
        top, rest = halves(jnp.concatenate([own, other], axis=0))
        face = face_of[slot]
        values = residual[slot]
        found = values - fast_dot(lift[slot], jnp.concatenate([top, rest, top], axis=0))
        search[slot] = found
        local = fast_dot(back[slot], jnp.concatenate(halves(found), axis=1))
        rhs[pl.ds(pl.multiple_of(face * FACE, FACE), FACE)] = local.astype(bf16)
        owned = is_owned((FACE, COLS), 0, lax.rem(face, 2))
        numerator += jnp.sum(jnp.where(owned, values * found, 0.0), axis=0, keepdims=True)

    def multiply(chunk, carry):
        rows = pl.ds(pl.multiple_of(chunk * CHUNK, CHUNK), CHUNK)
        both = fast_dot(high[rows], rhs[...]) + fast_dot(low[rows], rhs[...])
        local_product[rows] = both[:, 0:COLS] + both[:, COLS : 2 * COLS]
        return carry

    lax.fori_loop(0, ORDER // CHUNK, multiply, 0)
    denominator = jnp.zeros((1, COLS), f32)
    for slot in range(FACES):
        rows = pl.ds(pl.multiple_of(face_of[slot] * FACE, FACE), FACE)
        both = fast_dot(onehot[slot], jnp.concatenate(halves(local_product[rows]), axis=1))
        found = both[:, 0:COLS] + both[:, COLS : 2 * COLS]
        product[slot] = found
        if shares is not None:
            share = fast_dot(fold[slot], jnp.concatenate(halves(found), axis=1))
            share = share[:, 0:COLS] + share[:, COLS : 2 * COLS]
            shares[slot] = share[0 : 2 * MODES] + share[2 * MODES : 4 * MODES]
        denominator += jnp.sum(search[slot] * found, axis=0, keepdims=True)

    return jnp.concatenate([numerator, denominator, jnp.zeros((6, COLS), f32)], axis=0)


def share_out(ids, product, scalars, shares, applied, partial, to2, to3, scal):
    for slot in range(FACES):
        applied[slot][...] = product[slot]
    own_share = shares[0, 0:MODES]
    for slot in range(1, FACES):
        own_share += shares[slot, 0:MODES]
    for cluster in range(2):
        term = jnp.where(ids[6:7] == cluster, own_share, 0.0)
        for slot in (0, 1, 4, 5):
            term += jnp.where(ids[slot : slot + 1] == cluster, shares[slot, MODES : 2 * MODES], 0.0)
        partial[cluster * MODES : (cluster + 1) * MODES] = term
    partial[2 * MODES : 2 * MODES + 8] = scalars
    to2[0:MODES] = shares[2, MODES : 2 * MODES]
    to2[MODES : MODES + 8] = scalars
    to3[0:MODES] = shares[3, MODES : 2 * MODES]
    to3[MODES : MODES + 8] = scalars
    scal[...] = scalars


def first_kernel(
    load_p, modes_p, got0, got1, got2, got3, got45, own, coeff, coeff2, coeff3, onehot, back, high, low,
    residual, lift, fold, ids, search, ap0, ap1, ap2, ap3, ap45, partial, to2, to3, scal, rhs, local_product, shares, product,
):
    got = (got0, got1, got2, got3, got45.at[1], got45.at[0])
    face_of = faces_of_slots()
    ids[6:8] = own[0:2]
    for slot in range(FACES):
        side = lax.rem(face_of[slot], 2)
        residual[slot, rows_of(side)] = load_p[slot, rows_of(side)]
        residual[slot, rows_of(1 - side)] = -got[slot][0:HALF]
        owned = is_owned((MODES, FACE), 1, side)
        theirs = got[slot][HALF : HALF + MODES]
        here = jnp.where(owned, modes_p[slot], 0.0)
        there = jnp.where(owned, 0.0, -jnp.concatenate([theirs, theirs], axis=1))
        basis = jnp.concatenate([here, there], axis=0)
        fold[slot] = jnp.concatenate(halves(basis), axis=0)
        top, rest = halves(basis.T)
        lift[slot] = jnp.concatenate([top, top, rest], axis=1)
        ids[slot : slot + 1] = got[slot][HALF + MODES : HALF + MODES + 1]
    scalars = search_and_apply(
        residual, lift, fold, ids, coeff, coeff2, coeff3, onehot, back, high, low, search, rhs, local_product, shares, product
    )
    applied = (ap0, ap1, ap2, ap3, ap45.at[0], ap45.at[1])
    share_out(ids, product, scalars, shares, applied, partial, to2, to3, scal)


def update(residual_in, search_in, total_in, applied_in, got, alpha, residual, total):
    step_size = alpha[0:1]
    for slot in range(FACES):
        residual[slot] = residual_in[slot] - step_size * (applied_in[slot][...] - got[slot][...])
        moved = step_size * search_in[slot]
        total[slot] = moved if total_in is None else total_in[slot] + moved


def middle_kernel(
    residual_in, search_in, in0, in1, in2, in3, in45, got0, got1, got2, got3, got45, alpha,
    lift, fold, ids, coeff, coeff2, coeff3, onehot, back, high, low,
    residual, total, search, ap0, ap1, ap2, ap3, ap45, partial, to2, to3, scal, rhs, local_product, shares, product,
):
    got = (got0, got1, got2, got3, got45.at[1], got45.at[0])
    applied_in = (in0, in1, in2, in3, in45.at[0], in45.at[1])
    update(residual_in, search_in, None, applied_in, got, alpha, residual, total)
    scalars = search_and_apply(
        residual, lift, fold, ids, coeff, coeff2, coeff3, onehot, back, high, low, search, rhs, local_product, shares, product
    )
    applied = (ap0, ap1, ap2, ap3, ap45.at[0], ap45.at[1])
    share_out(ids, product, scalars, shares, applied, partial, to2, to3, scal)


def last_kernel(
    residual_in, search_in, total_in, in0, in1, in2, in3, in45, got0, got1, got2, got3, got45, alpha,
    lift, fold, ids, coeff, coeff2, coeff3, onehot, back, high, low,
    residual, total, search, product, ap0, ap1, ap2, ap3, ap45, scal, rhs, local_product,
):
    got = (got0, got1, got2, got3, got45.at[1], got45.at[0])
    applied_in = (in0, in1, in2, in3, in45.at[0], in45.at[1])
    update(residual_in, search_in, total_in, applied_in, got, alpha, residual, total)
    scal[...] = search_and_apply(
        residual, lift, fold, ids, coeff, coeff2, coeff3, onehot, back, high, low, search, rhs, local_product, None, product
    )
    face_of = faces_of_slots()
    for slot, sent in enumerate((ap0, ap1, ap2, ap3, ap45.at[0], ap45.at[1])):
        sent[...] = product[slot, rows_of(1 - lax.rem(face_of[slot], 2))]


def finish_kernel(
    residual_in, search_in, total_in, product, got0, got1, got2, got3, got45, sum0, sum1, sum2, sum3, back,
    total, residual, arrived,
):
    reduced = (sum0[...] + sum1[...]) + (sum2[...] + sum3[...])
    face_of = faces_of_slots()
    step_size = damping_factor * reduced[0:1] / reduced[1:2]
    for slot, values in enumerate((got0, got1, got2, got3, got45.at[1], got45.at[0])):
        arrived[slot] = jnp.concatenate([values[...], values[...]], axis=0)

    def one(slot, carry):
        face = face_of[slot]
        owned = is_owned((FACE, COLS), 0, lax.rem(face, 2))
        summed = total_in[slot] + step_size * search_in[slot]
        left = residual_in[slot] - step_size * (product[slot] - arrived[slot])
        total[face] = reorder(back[slot], jnp.where(owned, summed, 0.0))
        residual[face] = reorder(back[slot], jnp.where(owned, left, 0.0))
        return carry

    for slot in range(FACES):
        one(slot, 0)


in_vmem = pl.BlockSpec(memory_space=pltpu.VMEM)
in_smem = pl.BlockSpec(memory_space=pltpu.SMEM)


def call(kernel, args, outs, scratch=()):
    shapes = [out if isinstance(out, jax.ShapeDtypeStruct) else jax.ShapeDtypeStruct(out, f32) for out in outs]
    return pl.pallas_call(
        kernel,
        out_shape=shapes,
        in_specs=[in_smem if arg.shape == (1, 1) else in_vmem for arg in args],
        out_specs=[in_vmem for _ in shapes],
        scratch_shapes=list(scratch),
        compiler_params=pltpu.CompilerParams(vmem_limit_bytes=VMEM_LIMIT),
    )(*args)


def permuted(array, axis, target):
    return lax.ppermute(array, axis, [(i, target(i)) for i in range(lax.axis_size(axis))])


def flipped(array, axis, mask):
    return permuted(array, axis, lambda i: i ^ mask)


def terms_over_sub(array):
    count = lax.axis_size("sub")
    stride, stage = 1, 0
    while True:
        block = 4 * stride
        terms = [array] + [
            permuted(array, "sub", lambda i, turn=turn: i - i % block + (i % block + turn * stride) % block)
            for turn in (1, 2, 3)
        ]
        stage += 1
        if block == count:
            return terms
        array = (terms[0] + terms[1]) + (terms[2] + terms[3])
        stride = block


def exchange(sent0, sent1, sent2, sent3, sent45):
    count = lax.axis_size("sub")
    got0 = flipped(sent0, "sub", 1)
    got1 = permuted(sent1, "sub", lambda i: (i + 2 * (i % 2) - 1) % count)
    got2, got3 = flipped(sent2, "clus", 1), flipped(sent3, "clus", 3)
    got45 = flipped(sent45, "sub", count // 2)
    return got0, got1, got2, got3, got45


def per_device(load, dual_op, modes, face_map, cluster):
    pairing = face_map[0, 0]
    face_of = jnp.array(faces_of_slots())
    position = jnp.arange(FACE)
    natural = jnp.where(position < HALF, 2 * position, 2 * position - FACE + 1)
    plus = jnp.broadcast_to(pairing[:, None], (3, 2, FACE)).reshape(FACES, FACE)
    rows = jnp.where((face_of % 2 == 0)[:, None], plus, position[None])
    back = (rows[:, :, None] == natural[None, None, :]).astype(bf16)

    split = jax.ShapeDtypeStruct((ORDER, ORDER), bf16)
    wide, narrow = (FACES, FACE, COLS), (PACK, HALF)
    onehot, own, load_p, modes_p, *packs, payload = call(
        setup_kernel,
        (cluster, load[0, 0], modes[0, 0], pairing),
        [
            jax.ShapeDtypeStruct((FACES, FACE, FACE), bf16),
            (8, COLS),
            wide,
            (FACES, MODES, FACE),
            narrow,
            narrow,
            narrow,
            narrow,
            (2, *narrow),
            (3 * MODES, COLS),
        ],
        [pltpu.VMEM((FACES, *narrow), f32)],
    )
    high, low = pl.pallas_call(
        split_kernel,
        out_shape=[split, split],
        grid=(FACES,),
        in_specs=[pl.BlockSpec((FACE, ORDER), lambda i: (i, 0))],
        out_specs=[pl.BlockSpec((FACE, ORDER), lambda i: (i, 0))] * 2,
        compiler_params=pltpu.CompilerParams(vmem_limit_bytes=VMEM_LIMIT),
        name="split_kernel",
    )(dual_op[0, 0])
    coeff_shape, one = (2 * MODES, COLS), (MODES, COLS)
    got = exchange(*packs)
    terms = terms_over_sub(payload)
    inverses, gathered, coeff, own_coeff = call(
        invert_kernel, (*terms, own), [one, coeff_shape, coeff_shape, one]
    )
    coeff2, coeff3 = flipped(own_coeff, "clus", 1), flipped(own_coeff, "clus", 3)

    face = (FACE, COLS)
    faces = [face, face, face, face, (2, *face)]
    sums = [(2 * MODES + 8, COLS), (MODES + 8, COLS), (MODES + 8, COLS), (8, COLS)]
    scratch = [
        pltpu.VMEM((ORDER, 2 * COLS), bf16),
        pltpu.VMEM((ORDER, COLS), f32),
        pltpu.VMEM((FACES, 2 * MODES, COLS), f32),
        pltpu.VMEM(wide, f32),
    ]
    residual, lift, fold, ids, search, *rest = call(
        first_kernel,
        (load_p, modes_p, *got, own, coeff, coeff2, coeff3, onehot, back, high, low),
        [
            wide,
            jax.ShapeDtypeStruct((FACES, FACE, 6 * MODES), bf16),
            jax.ShapeDtypeStruct((FACES, 4 * MODES, FACE), bf16),
            (8, COLS),
            wide,
            *faces,
            *sums,
        ],
        scratch,
    )
    total = None
    for iteration in (1, 2):
        applied, (partial, to2, to3, scal) = rest[:5], rest[5:]
        got = exchange(*applied)
        got2, got3, across = flipped(to2, "clus", 1), flipped(to3, "clus", 3), flipped(scal, "clus", 2)
        (payload,) = call(combine_kernel, (partial, got2, got3, across, own), [sums[0]])
        terms = terms_over_sub(payload)
        alpha, gathered, coeff, own_coeff = call(
            step_kernel,
            (*terms, gathered, inverses, own),
            [(8, COLS), coeff_shape, coeff_shape, one],
        )
        coeff2, coeff3 = flipped(own_coeff, "clus", 1), flipped(own_coeff, "clus", 3)
        common = (*applied, *got, alpha, lift, fold, ids, coeff, coeff2, coeff3, onehot, back, high, low)
        if iteration == 1:
            residual, total, search, *rest = call(
                middle_kernel, (residual, search, *common), [wide, wide, wide, *faces, *sums], scratch
            )
        else:
            half = (HALF, COLS)
            residual, total, search, product, *rest = call(
                last_kernel,
                (residual, search, total, *common),
                [wide, wide, wide, wide, half, half, half, half, (2, *half), (8, COLS)],
                scratch[:2],
            )
    got = exchange(*rest[:5])
    scal = rest[5]
    scal = scal + flipped(scal, "clus", 1)
    scal = scal + flipped(scal, "clus", 2)
    terms = terms_over_sub(scal)
    total, residual = call(
        finish_kernel,
        (residual, search, total, product, *got, *terms, back),
        [wide, wide],
        [pltpu.VMEM(wide, f32)],
    )
    return (total[None, None], residual[None, None])


def solution(mesh):
    placed = (
        P("clus", "sub", None, None, None),
        P("clus", "sub", None, None),
        P("clus", "sub", None, None),
        P("clus", "sub", None, None),
        P("clus", "sub"),
    )
    return jax.shard_map(
        per_device,
        mesh=mesh,
        in_specs=placed,
        out_specs=(P("clus", "sub", None, None, None), P("clus", "sub", None, None, None)),
        check_vma=False,
    )
```

```python
import jax
import jax.numpy as jnp
from jax import lax
from jax.experimental import pallas as pl
from jax.experimental.pallas import tpu as pltpu
from jax.sharding import PartitionSpec as P

FACE = 256
HALF = 128
COLS = 128
MODES = 32
ORDER = 1536
FACES = 6
VMEM_LIMIT = 16 << 20
CHUNK = 768
PACK = HALF + MODES + 8

TAIL = slice(MODES + 8, MODES + 8 + FACE)
NEAR_TAIL = slice(2 * MODES + 8, 2 * MODES + 8 + FACE)

damping_factor = 0.8
f32 = jnp.float32
bf16 = jnp.bfloat16


def exact_dot(a, b, contract=((1,), (0,))):
    return lax.dot_general(
        a, b, (contract, ((), ())), precision=lax.Precision.HIGHEST, preferred_element_type=f32
    )


def fast_dot(a, b, contract=((1,), (0,))):
    return lax.dot_general(a, b, (contract, ((), ())), preferred_element_type=f32)


def split3(x):
    high = x.astype(bf16)
    rest = x - high.astype(f32)
    middle = rest.astype(bf16)
    low = (rest - middle.astype(f32)).astype(bf16)
    return high, middle, low


def reorder(onehot, x):
    high, middle, low = split3(x)
    return fast_dot(onehot, high) + fast_dot(onehot, middle) + fast_dot(onehot, low)


def rows_of(side):
    return pl.ds(pl.multiple_of(side * HALF, HALF), HALF)


def is_owned(shape, axis, side):
    return lax.broadcasted_iota(jnp.int32, shape, axis) // HALF == side


def faces_of_slots():
    odd_sub = lax.rem(lax.axis_index("sub"), 2)
    odd_clus = lax.rem(lax.axis_index("clus"), 2)
    return [odd_sub, 1 - odd_sub, 2 + odd_clus, 3 - odd_clus, 4, 5]


def split_kernel(operator, high, low):
    values = operator[...]
    rounded = values.astype(bf16)
    high[...] = rounded
    low[...] = (values - rounded.astype(f32)).astype(bf16)


def setup_kernel(
    cluster, load, modes, pairing, onehot, own, load_p, modes_p, pack0, pack1, pack2, pack3, pack45, payload, packs
):
    face_of = faces_of_slots()
    own[...] = jnp.full((8, COLS), cluster[0, 0]).astype(f32)
    row = lax.broadcasted_iota(jnp.int32, (FACE, FACE), 0)
    lane = lax.broadcasted_iota(jnp.int32, (FACE, FACE), 1)
    natural = jnp.where(row < HALF, 2 * row, 2 * row - FACE + 1)

    def one(slot, carry):
        gram, projected = carry
        face = face_of[slot]
        side = lax.rem(face, 2)
        plus = jnp.broadcast_to(pairing[slot // 2 : slot // 2 + 1], (FACE, FACE))
        target = jnp.where(jnp.full((FACE, FACE), side) == 0, plus, lane)
        onehot[slot] = (target == natural).astype(bf16)
        load_p[slot] = reorder(onehot[slot], load[face])
        parts = split3(modes[:, pl.ds(pl.multiple_of(face * FACE, FACE), FACE)])
        rows = sum(fast_dot(part, onehot[slot], ((1,), (1,))) for part in parts)
        modes_p[slot] = rows
        mine = jnp.where(jnp.full((MODES, HALF), side) == 0, rows[:, :HALF], rows[:, HALF:])
        values = load_p[slot, rows_of(side)]
        packs[slot, 0:HALF] = values
        packs[slot, HALF : HALF + MODES] = mine
        packs[slot, HALF + MODES : PACK] = own[...]
        return gram + exact_dot(mine, mine, ((1,), (1,))), projected + exact_dot(mine, values)

    gram, projected = jnp.zeros((MODES, MODES), f32), jnp.zeros((MODES, COLS), f32)
    for slot in range(FACES):
        gram, projected = one(slot, (gram, projected))
    for slot, pack in enumerate((pack0.at[3 * MODES : 3 * MODES + PACK], pack1, pack2, pack3, pack45.at[0], pack45.at[1])):
        pack[...] = packs[slot]
    own_row = own[0:1]
    payload[0:MODES] = jnp.where(own_row == 0.0, projected, 0.0)
    payload[MODES : 2 * MODES] = jnp.where(own_row == 1.0, projected, 0.0)
    lane = lax.broadcasted_iota(jnp.int32, (MODES, COLS), 1)
    row = lax.broadcasted_iota(jnp.int32, (MODES, COLS), 0)
    place = (lane == row + MODES * own_row.astype(jnp.int32)).astype(f32)
    payload[2 * MODES : 3 * MODES] = exact_dot(gram, place)
    pack0[0 : 3 * MODES] = payload[...]


def solve_both(inverses, gathered, own_row, coeff, own_coeff):
    zero = jnp.zeros((MODES, COLS), f32)
    first = exact_dot(inverses, jnp.concatenate([zero, zero, gathered[0:MODES], zero], axis=0))
    second = exact_dot(inverses, jnp.concatenate([zero, zero, zero, gathered[MODES : 2 * MODES]], axis=0))
    coeff[0:MODES] = first
    coeff[MODES : 2 * MODES] = second
    own_coeff[...] = jnp.where(own_row == 0.0, first, second)


def invert_kernel(sum0, sum1, sum2, sum3, own, inverses, gathered, coeff, own_coeff):
    reduced = (sum0[...] + sum1[...]) + (sum2[...] + sum3[...])
    lane = lax.broadcasted_iota(jnp.int32, (MODES, COLS), 1)
    row = lax.broadcasted_iota(jnp.int32, (MODES, COLS), 0)
    work = reduced[2 * MODES : 3 * MODES]
    work = jnp.where(lane < 2 * MODES, work, (lane % MODES == row).astype(f32))
    second = (lane // MODES) % 2 == 1
    for step in range(MODES):
        column = jnp.where(
            second,
            jnp.broadcast_to(work[:, MODES + step : MODES + step + 1], (MODES, COLS)),
            jnp.broadcast_to(work[:, step : step + 1], (MODES, COLS)),
        )
        scaled = work[step : step + 1] / column[step : step + 1]
        work = jnp.where(row == step, scaled, work - column * scaled)
    inverses[...] = work
    gathered[...] = reduced[0 : 2 * MODES]
    solve_both(work, reduced[0 : 2 * MODES], own[0:1], coeff, own_coeff)


def combine_kernel(partial, got2, got3, across, own, sent0, payload, near):
    head = slice(0, MODES + 8)
    arrived = got2[head] + got3[head]
    own_row = own[0:1]
    for slot in range(2):
        rows = slice(slot * MODES, (slot + 1) * MODES)
        payload[rows] = partial[rows] + jnp.where(own_row == slot, arrived[0:MODES], 0.0)
    tail = slice(2 * MODES, 2 * MODES + 8)
    payload[tail] = (partial[tail] + across[...]) + arrived[MODES : MODES + 8]
    near[0 : 2 * MODES + 8] = payload[...]
    near[NEAR_TAIL] = sent0[...]


def step_kernel(sum0, sum1, sum2, sum3, gathered, inverses, own, alpha, gathered_out, coeff, own_coeff):
    reduced = (sum0[...] + sum1[...]) + (sum2[...] + sum3[...])
    step_size = damping_factor * reduced[64:65] / reduced[65:66]
    alpha[...] = jnp.broadcast_to(step_size, (8, COLS))
    updated = gathered[0 : 2 * MODES] - step_size * reduced[0 : 2 * MODES]
    gathered_out[...] = updated
    solve_both(inverses[...], updated, own[0:1], coeff, own_coeff)


def halves(x):
    top = x.astype(bf16)
    return top, (x - top.astype(f32)).astype(bf16)


def search_and_apply(
    residual, lift, fold, ids, coeff, coeff2, coeff3, onehot, back, high, low, search, rhs, local_product, shares, product
):
    face_of = faces_of_slots()
    own_row = ids[6:7]
    own = jnp.where(own_row == 0.0, coeff[0:MODES], coeff[MODES : 2 * MODES])
    numerator = jnp.zeros((1, COLS), f32)
    for slot in range(FACES):
        if slot == 2:
            other = coeff2[...]
        elif slot == 3:
            other = coeff3[...]
        else:
            other = jnp.where(ids[slot : slot + 1] == 0.0, coeff[0:MODES], coeff[MODES : 2 * MODES])
        top, rest = halves(jnp.concatenate([own, other], axis=0))
        face = face_of[slot]
        values = residual[slot]
        found = values - fast_dot(lift[slot], jnp.concatenate([top, rest, top], axis=0))
        search[slot] = found
        local = fast_dot(back[slot], jnp.concatenate(halves(found), axis=1))
        rhs[pl.ds(pl.multiple_of(face * FACE, FACE), FACE)] = local.astype(bf16)
        owned = is_owned((FACE, COLS), 0, lax.rem(face, 2))
        numerator += jnp.sum(jnp.where(owned, values * found, 0.0), axis=0, keepdims=True)

    def multiply(chunk, carry):
        rows = pl.ds(pl.multiple_of(chunk * CHUNK, CHUNK), CHUNK)
        both = fast_dot(high[rows], rhs[...]) + fast_dot(low[rows], rhs[...])
        local_product[rows] = both[:, 0:COLS] + both[:, COLS : 2 * COLS]
        return carry

    lax.fori_loop(0, ORDER // CHUNK, multiply, 0)
    denominator = jnp.zeros((1, COLS), f32)
    for slot in range(FACES):
        rows = pl.ds(pl.multiple_of(face_of[slot] * FACE, FACE), FACE)
        both = fast_dot(onehot[slot], jnp.concatenate(halves(local_product[rows]), axis=1))
        found = both[:, 0:COLS] + both[:, COLS : 2 * COLS]
        product[slot] = found
        if shares is not None:
            share = fast_dot(fold[slot], jnp.concatenate(halves(found), axis=1))
            share = share[:, 0:COLS] + share[:, COLS : 2 * COLS]
            shares[slot] = share[0 : 2 * MODES] + share[2 * MODES : 4 * MODES]
        denominator += jnp.sum(search[slot] * found, axis=0, keepdims=True)

    return jnp.concatenate([numerator, denominator, jnp.zeros((6, COLS), f32)], axis=0)


def share_out(ids, product, scalars, shares, applied, partial, to2, to3, scal):
    for slot in range(FACES):
        applied[slot][...] = product[slot]
    own_share = shares[0, 0:MODES]
    for slot in range(1, FACES):
        own_share += shares[slot, 0:MODES]
    for cluster in range(2):
        term = jnp.where(ids[6:7] == cluster, own_share, 0.0)
        for slot in (0, 1, 4, 5):
            term += jnp.where(ids[slot : slot + 1] == cluster, shares[slot, MODES : 2 * MODES], 0.0)
        partial[cluster * MODES : (cluster + 1) * MODES] = term
    partial[2 * MODES : 2 * MODES + 8] = scalars
    to2[0:MODES] = shares[2, MODES : 2 * MODES]
    to2[MODES : MODES + 8] = scalars
    to3[0:MODES] = shares[3, MODES : 2 * MODES]
    to3[MODES : MODES + 8] = scalars
    scal[...] = scalars


def first_kernel(
    load_p, modes_p, got0, got1, got2, got3, got45, own, coeff, coeff2, coeff3, onehot, back, high, low,
    residual, lift, fold, ids, search, ap0, ap1, to2, to3, ap45, partial, scal, rhs, local_product, shares, product,
):
    got = (got0.at[3 * MODES : 3 * MODES + PACK], got1, got2, got3, got45.at[1], got45.at[0])
    face_of = faces_of_slots()
    ids[6:8] = own[0:2]
    for slot in range(FACES):
        side = lax.rem(face_of[slot], 2)
        residual[slot, rows_of(side)] = load_p[slot, rows_of(side)]
        residual[slot, rows_of(1 - side)] = -got[slot][0:HALF]
        owned = is_owned((MODES, FACE), 1, side)
        theirs = got[slot][HALF : HALF + MODES]
        here = jnp.where(owned, modes_p[slot], 0.0)
        there = jnp.where(owned, 0.0, -jnp.concatenate([theirs, theirs], axis=1))
        basis = jnp.concatenate([here, there], axis=0)
        fold[slot] = jnp.concatenate(halves(basis), axis=0)
        top, rest = halves(basis.T)
        lift[slot] = jnp.concatenate([top, top, rest], axis=1)
        ids[slot : slot + 1] = got[slot][HALF + MODES : HALF + MODES + 1]
    scalars = search_and_apply(
        residual, lift, fold, ids, coeff, coeff2, coeff3, onehot, back, high, low, search, rhs, local_product, shares, product
    )
    applied = (ap0, ap1, to2.at[TAIL], to3.at[TAIL], ap45.at[0], ap45.at[1])
    share_out(ids, product, scalars, shares, applied, partial, to2, to3, scal)


def update(residual_in, search_in, total_in, applied_in, got, alpha, residual, total):
    step_size = alpha[0:1]
    for slot in range(FACES):
        residual[slot] = residual_in[slot] - step_size * (applied_in[slot][...] - got[slot][...])
        moved = step_size * search_in[slot]
        total[slot] = moved if total_in is None else total_in[slot] + moved


def middle_kernel(
    residual_in, search_in, in0, in1, in2, in3, in45, got0, got1, got2, got3, got45, alpha,
    lift, fold, ids, coeff, coeff2, coeff3, onehot, back, high, low,
    residual, total, search, ap0, ap1, to2, to3, ap45, partial, scal, rhs, local_product, shares, product,
):
    got = (got0.at[NEAR_TAIL], got1, got2.at[TAIL], got3.at[TAIL], got45.at[1], got45.at[0])
    applied_in = (in0, in1, in2.at[TAIL], in3.at[TAIL], in45.at[0], in45.at[1])
    update(residual_in, search_in, None, applied_in, got, alpha, residual, total)
    scalars = search_and_apply(
        residual, lift, fold, ids, coeff, coeff2, coeff3, onehot, back, high, low, search, rhs, local_product, shares, product
    )
    applied = (ap0, ap1, to2.at[TAIL], to3.at[TAIL], ap45.at[0], ap45.at[1])
    share_out(ids, product, scalars, shares, applied, partial, to2, to3, scal)


def last_kernel(
    residual_in, search_in, total_in, in0, in1, in2, in3, in45, got0, got1, got2, got3, got45, alpha,
    lift, fold, ids, coeff, coeff2, coeff3, onehot, back, high, low,
    residual, total, search, product, ap0, ap1, ap2, ap3, ap45, scal, rhs, local_product,
):
    got = (got0.at[NEAR_TAIL], got1, got2.at[TAIL], got3.at[TAIL], got45.at[1], got45.at[0])
    applied_in = (in0, in1, in2.at[TAIL], in3.at[TAIL], in45.at[0], in45.at[1])
    update(residual_in, search_in, total_in, applied_in, got, alpha, residual, total)
    scalars = search_and_apply(
        residual, lift, fold, ids, coeff, coeff2, coeff3, onehot, back, high, low, search, rhs, local_product, None, product
    )
    face_of = faces_of_slots()
    scal[...] = scalars
    ap2[HALF : HALF + 8] = scalars
    ap3[HALF : HALF + 8] = scalars
    for slot, sent in enumerate((ap0, ap1, ap2.at[0:HALF], ap3.at[0:HALF], ap45.at[0], ap45.at[1])):
        sent[...] = product[slot, rows_of(1 - lax.rem(face_of[slot], 2))]


def finish_kernel(
    residual_in, search_in, total_in, product, got0, got1, got2, got3, got45, sum0, sum1, sum2, sum3, back,
    total, residual, arrived,
):
    reduced = (sum0[...] + sum1[...]) + (sum2[...] + sum3[...])
    face_of = faces_of_slots()
    step_size = damping_factor * reduced[0:1] / reduced[1:2]
    for slot, values in enumerate((got0, got1, got2.at[0:HALF], got3.at[0:HALF], got45.at[1], got45.at[0])):
        arrived[slot] = jnp.concatenate([values[...], values[...]], axis=0)

    def one(slot, carry):
        face = face_of[slot]
        owned = is_owned((FACE, COLS), 0, lax.rem(face, 2))
        summed = total_in[slot] + step_size * search_in[slot]
        left = residual_in[slot] - step_size * (product[slot] - arrived[slot])
        total[face] = reorder(back[slot], jnp.where(owned, summed, 0.0))
        residual[face] = reorder(back[slot], jnp.where(owned, left, 0.0))
        return carry

    for slot in range(FACES):
        one(slot, 0)


in_vmem = pl.BlockSpec(memory_space=pltpu.VMEM)
in_smem = pl.BlockSpec(memory_space=pltpu.SMEM)


def call(kernel, args, outs, scratch=()):
    shapes = [out if isinstance(out, jax.ShapeDtypeStruct) else jax.ShapeDtypeStruct(out, f32) for out in outs]
    return pl.pallas_call(
        kernel,
        out_shape=shapes,
        in_specs=[in_smem if arg.shape == (1, 1) else in_vmem for arg in args],
        out_specs=[in_vmem for _ in shapes],
        scratch_shapes=list(scratch),
        compiler_params=pltpu.CompilerParams(vmem_limit_bytes=VMEM_LIMIT),
    )(*args)


def permuted(array, axis, target):
    return lax.ppermute(array, axis, [(i, target(i)) for i in range(lax.axis_size(axis))])


def flipped(array, axis, mask):
    return permuted(array, axis, lambda i: i ^ mask)


def terms_over_sub(array, near=None):
    count = lax.axis_size("sub")
    stride, stage, arrived = 1, 0, None
    while True:
        terms = [array]
        for turn in (1, 3, 2):
            if near is not None and stage == 0 and turn == 1:
                arrived = flipped(near, "sub", 1)
                terms.append(arrived[: array.shape[0]])
            else:
                terms.append(flipped(array, "sub", turn * stride))
        if 4 * stride == count:
            return terms, arrived
        array = (terms[0] + terms[1]) + (terms[2] + terms[3])
        stride *= 4
        stage += 1


def far_exchange(sent1, sent45):
    count = lax.axis_size("sub")
    got1 = permuted(sent1, "sub", lambda i: (i + 2 * (i % 2) - 1) % count)
    got45 = flipped(sent45, "sub", count // 2)
    return got1, got45


def across_faces(sent2, sent3):
    return flipped(sent2, "clus", 1), flipped(sent3, "clus", 3)


def per_device(load, dual_op, modes, face_map, cluster):
    pairing = face_map[0, 0]
    face_of = jnp.array(faces_of_slots())
    position = jnp.arange(FACE)
    natural = jnp.where(position < HALF, 2 * position, 2 * position - FACE + 1)
    plus = jnp.broadcast_to(pairing[:, None], (3, 2, FACE)).reshape(FACES, FACE)
    rows = jnp.where((face_of % 2 == 0)[:, None], plus, position[None])
    back = (rows[:, :, None] == natural[None, None, :]).astype(bf16)

    split = jax.ShapeDtypeStruct((ORDER, ORDER), bf16)
    wide, narrow = (FACES, FACE, COLS), (PACK, HALF)
    onehot, own, load_p, modes_p, *packs, payload = call(
        setup_kernel,
        (cluster, load[0, 0], modes[0, 0], pairing),
        [
            jax.ShapeDtypeStruct((FACES, FACE, FACE), bf16),
            (8, COLS),
            wide,
            (FACES, MODES, FACE),
            (3 * MODES + PACK, HALF),
            narrow,
            narrow,
            narrow,
            (2, *narrow),
            (3 * MODES, COLS),
        ],
        [pltpu.VMEM((FACES, *narrow), f32)],
    )
    coeff_shape, one = (2 * MODES, COLS), (MODES, COLS)
    high, low = pl.pallas_call(
        split_kernel,
        out_shape=[split, split],
        grid=(FACES,),
        in_specs=[pl.BlockSpec((FACE, ORDER), lambda i: (i, 0))],
        out_specs=[pl.BlockSpec((FACE, ORDER), lambda i: (i, 0))] * 2,
        compiler_params=pltpu.CompilerParams(vmem_limit_bytes=VMEM_LIMIT),
        name="split_kernel",
    )(pltpu.with_memory_space_constraint(dual_op[0, 0], pltpu.HBM))
    got1, got45 = far_exchange(packs[1], packs[4])
    got2, got3 = across_faces(packs[2], packs[3])
    terms, got0 = terms_over_sub(payload, packs[0])
    got = got0, got1, got2, got3, got45
    inverses, gathered, coeff, own_coeff = call(
        invert_kernel, (*terms, own), [one, coeff_shape, coeff_shape, one]
    )
    coeff2, coeff3 = flipped(own_coeff, "clus", 1), flipped(own_coeff, "clus", 3)

    face = (FACE, COLS)
    wider = (MODES + 8 + FACE, COLS)
    faces = [face, face, wider, wider, (2, *face)]
    sums = [(2 * MODES + 8, COLS), (8, COLS)]
    scratch = [
        pltpu.VMEM((ORDER, 2 * COLS), bf16),
        pltpu.VMEM((ORDER, COLS), f32),
        pltpu.VMEM((FACES, 2 * MODES, COLS), f32),
        pltpu.VMEM(wide, f32),
    ]
    residual, lift, fold, ids, search, *rest = call(
        first_kernel,
        (load_p, modes_p, *got, own, coeff, coeff2, coeff3, onehot, back, high, low),
        [
            wide,
            jax.ShapeDtypeStruct((FACES, FACE, 6 * MODES), bf16),
            jax.ShapeDtypeStruct((FACES, 4 * MODES, FACE), bf16),
            (8, COLS),
            wide,
            *faces,
            *sums,
        ],
        scratch,
    )
    total = None
    for iteration in (1, 2):
        applied, (partial, scal) = rest[:5], rest[5:]
        got2, got3 = across_faces(applied[2], applied[3])
        across = flipped(scal, "clus", 2)
        payload, near = call(
            combine_kernel,
            (partial, got2, got3, across, own, applied[0]),
            [sums[0], (2 * MODES + 8 + FACE, COLS)],
        )
        got1, got45 = far_exchange(applied[1], applied[4])
        terms, got0 = terms_over_sub(payload, near)
        got = got0, got1, got2, got3, got45
        alpha, gathered, coeff, own_coeff = call(
            step_kernel,
            (*terms, gathered, inverses, own),
            [(8, COLS), coeff_shape, coeff_shape, one],
        )
        coeff2, coeff3 = flipped(own_coeff, "clus", 1), flipped(own_coeff, "clus", 3)
        common = (*applied, *got, alpha, lift, fold, ids, coeff, coeff2, coeff3, onehot, back, high, low)
        if iteration == 1:
            residual, total, search, *rest = call(
                middle_kernel, (residual, search, *common), [wide, wide, wide, *faces, *sums], scratch
            )
        else:
            half, longer = (HALF, COLS), (HALF + 8, COLS)
            residual, total, search, product, *rest = call(
                last_kernel,
                (residual, search, total, *common),
                [wide, wide, wide, wide, half, half, longer, longer, (2, *half), (8, COLS)],
                scratch[:2],
            )
    sent0, sent1, sent2, sent3, sent45, scal = rest
    got2, got3 = across_faces(sent2, sent3)
    scal = (scal + flipped(scal, "clus", 2)) + (got2[HALF:] + got3[HALF:])
    got1, got45 = far_exchange(sent1, sent45)
    got0 = flipped(sent0, "sub", 1)
    terms, _ = terms_over_sub(scal)
    got = got0, got1, got2, got3, got45
    total, residual = call(
        finish_kernel,
        (residual, search, total, product, *got, *terms, back),
        [wide, wide],
        [pltpu.VMEM(wide, f32)],
    )
    return (total[None, None], residual[None, None])


def solution(mesh):
    placed = (
        P("clus", "sub", None, None, None),
        P("clus", "sub", None, None),
        P("clus", "sub", None, None),
        P("clus", "sub", None, None),
        P("clus", "sub"),
    )
    return jax.shard_map(
        per_device,
        mesh=mesh,
        in_specs=placed,
        out_specs=(P("clus", "sub", None, None, None), P("clus", "sub", None, None, None)),
        check_vma=False,
    )
```
